32 devices in a mesh: frame: 8 (over z, core), tok: 4 (over y, x).
Axes of the slice: x: 2, y: 2, z: 4, core: 2. Of those that a mesh axis runs over, the one named last changes fastest.
Arguments:
- stream: bfloat16 [8, 1024, 1152], P('frame', 'tok'), may hold values from -20 to 20
- queries: bfloat16 [8, 1024, 1152], P('frame', 'tok'), may hold values from -200 to 200
- key_vectors: bfloat16 [8, 1024, 1152], P('frame', 'tok'), may hold values from -6 to 6
- value_vectors: bfloat16 [8, 1024, 1152], P('frame', 'tok'), may hold values from -6 to 6
- modulation: float32 [8, 4, 1152], P('frame'), may hold values from -4 to 4
- output_weight: bfloat16 [1152, 1152], replicated, may hold values from -0.1875 to 0.1875
- output_bias: float32 [1152], replicated, may hold values from -3 to 3
- router_weight: bfloat16 [1152, 8], replicated, may hold values from -0.1875 to 0.1875
- expand_weight: bfloat16 [8, 1152, 4608], P('frame', None, 'tok'), may hold values from -0.1875 to 0.1875
- expand_bias: float32 [8, 4608], P('frame', 'tok'), may hold values from -3 to 3
- reduce_weight: bfloat16 [8, 4608, 1152], P('frame', 'tok'), may hold values from -0.09375 to 0.09375
- reduce_bias: float32 [8, 1152], P('frame'), may hold values from -3 to 3
- counts: int32 [8, 8], P(None, 'frame'), may hold values from 1 to 96, 256 in all within a row
- picked_rows: int32 [8, 8, 96], P(None, 'frame'), may hold values from 0 to 1023, as said below
Outputs:
- layer_out: bfloat16 [8, 1024, 1152], P('frame', 'tok')
The draws below stay inside these ranges and needn't reach their ends.
Inputs may be any that keep to these rules, and one draw needn't show every extreme that they name: counts[e, g] slots of block (e, g) are used; the counts of one expert sum to 256. The entries of one block picked_rows[e, g, :] are distinct positions among the 1024 tokens of frame g; slots at or beyond counts[e, g] are unused.
All inputs are finite; a program needn't handle non-finite values.
Results may differ from the reference program's by a relative error of at most 0.0055.
Values may be sent and summed in bfloat16 or wider, within the bound.
A program may use at most 64 MiB of HBM per device.

```python
import math
import jax
import jax.numpy as jnp
import numpy as np
from jax import lax

D = 1152
H = 16
HD = 72
FF = 4608
CAP = 256
FTOK = 1024
FRAMES = 8
EXPERTS = 8
BLK = 96
N_FRAME = 8


def draw_stream(key, part):
    first_key, second_key = jax.random.split(key, 2)
    column_scale = jnp.exp(jax.random.uniform(second_key, (1, 1, D), jnp.float32, math.log(0.3), math.log(3.0)))
    values = jax.random.normal(first_key, (FRAMES, FTOK, D), jnp.float32) * column_scale
    return jnp.clip(values, -20.0, 20.0).astype(jnp.bfloat16)


def drawn_pair(key):
    key_draw = jnp.clip(jax.random.normal(jax.random.fold_in(key, 17), (FRAMES, FTOK, D), jnp.float32), -6.0, 6.0)
    query_draw = jnp.clip(2.5 * jax.random.normal(jax.random.fold_in(key, 29), (FRAMES, FTOK, D), jnp.float32), -15.0, 15.0)
    return (query_draw, key_draw)


def draw_queries(key, part):
    query_draw, key_draw = drawn_pair(key)
    return query_draw.astype(jnp.bfloat16)


def draw_key_vectors(key, part):
    query_draw, key_draw = drawn_pair(key)
    return key_draw.astype(jnp.bfloat16)


def draw_picked_rows(key, part):
    block_keys = jax.random.split(key, EXPERTS * N_FRAME)

    def one_block(block_key):
        return jax.random.permutation(block_key, FTOK)[:BLK].astype(jnp.int32)
    picked = jax.vmap(one_block)(block_keys).reshape(EXPERTS, N_FRAME, BLK)
    upper = (picked[0, 0] - picked[0, 0, 0] + FTOK - 1) % FTOK
    lower = (picked[0, 1] - picked[0, 1, 0]) % FTOK
    picked = picked.at[0, 0].set(upper.astype(jnp.int32))
    picked = picked.at[0, 1].set(lower.astype(jnp.int32))
    return picked.astype(jnp.int32)


def block_levels(own_key, shape, shards, least, high):
    def one(axis_at, shards_of):
        steps = jax.random.uniform(jax.random.fold_in(jax.random.fold_in(own_key, 6), axis_at), (shards_of,), jnp.float32, least / len(shards), high / len(shards))
        return jnp.repeat(jnp.exp(steps), shape[axis_at] // shards_of).reshape((-1,) + (1,) * (len(shape) - axis_at - 1))

    level = one(*shards[0])
    for cut in shards[1:]:
        level = level * one(*cut)
    return level


def split_up(count, total, bound, slope):
    portions = [(1 << 20) // math.isqrt(rank ** slope) + 1 for rank in range(2, count + 1)]
    rest, given = total - bound - (count - 1), [1] * (count - 1)
    while rest > 0:
        free = [i for i in range(count - 1) if given[i] < bound]
        whole, budget = sum([portions[i] for i in free]), rest
        for i in free:
            more = min(bound - given[i], max(1, budget * portions[i] // whole), rest)
            given[i] = given[i] + more
            rest = rest - more
    return np.array([bound] + given)


def ragged_sizes(own_key, number_of, total, most, lean):
    if number_of == 2:
        one = jax.random.randint(own_key, (), max(1, total - most), min(most, total - 1) + 1)
        return jnp.stack([one, total - one])
    lengths = jnp.asarray(split_up(number_of, total, most, lean), jnp.int32)
    twos = (number_of - 1) // 2
    donor, receiver = lengths[1:1 + 2 * twos:2], lengths[2:2 + 2 * twos:2]
    room = jnp.minimum(donor - 1, most - receiver)
    passed = jax.random.randint(jax.random.fold_in(own_key, 1), (twos,), 0, 1 << 20) % (room + 1)
    lengths = lengths.at[1:1 + 2 * twos:2].set(donor - passed).at[2:2 + 2 * twos:2].set(receiver + passed)
    return lengths[jax.random.permutation(jax.random.fold_in(own_key, 2), number_of)]


def noise(own_key, shape, spread, most, cuts=(), kind=jnp.bfloat16):
    array = spread * jax.random.normal(own_key, shape, jnp.float32)
    if cuts:
        array = array * block_levels(own_key, shape, cuts, -0.22, 0.18)
    return jnp.clip(array, -most, most).astype(kind)


def setup_inputs(seed: int = 0) -> dict:
    keys = jax.random.split(jax.random.key(seed), 15)
    stream = draw_stream(jax.random.fold_in(keys[14], 71), 0)
    queries = draw_queries(jax.random.fold_in(keys[14], 71), 0)
    key_vectors = draw_key_vectors(jax.random.fold_in(keys[14], 71), 0)
    value_vectors = noise(keys[3], (FRAMES, FTOK, D), 1.0, 6.0, ((0, 8), (1, 4)))
    modulation = noise(keys[4], (FRAMES, 4, D), 1.0, 4.0, ((0, 8),), jnp.float32)
    output_weight = noise(keys[5], (D, D), D ** -0.5, 0.1875)
    output_bias = noise(keys[6], (D,), 0.5, 3.0, (), jnp.float32)
    router_weight = noise(keys[7], (D, EXPERTS), D ** -0.5, 0.1875)
    expand_weight = noise(keys[8], (EXPERTS, D, FF), D ** -0.5, 0.1875, ((0, 8), (2, 4)))
    expand_bias = noise(keys[9], (EXPERTS, FF), 0.5, 3.0, ((0, 8), (1, 4)), jnp.float32)
    reduce_weight = noise(keys[10], (EXPERTS, FF, D), FF ** -0.5, 0.09375, ((0, 8), (1, 4)))
    reduce_bias = noise(keys[11], (EXPERTS, D), 0.5, 3.0, ((0, 8),), jnp.float32)
    counts = jax.vmap(lambda own: ragged_sizes(own, N_FRAME, CAP, BLK, 2))(jax.random.split(keys[12], EXPERTS)).reshape((EXPERTS, N_FRAME)).astype(jnp.int32)
    picked_rows = draw_picked_rows(jax.random.fold_in(keys[14], 71), 0)
    return {"stream": stream, "queries": queries, "key_vectors": key_vectors, "value_vectors": value_vectors, "modulation": modulation, "output_weight": output_weight, "output_bias": output_bias, "router_weight": router_weight, "expand_weight": expand_weight, "expand_bias": expand_bias, "reduce_weight": reduce_weight, "reduce_bias": reduce_bias, "counts": counts, "picked_rows": picked_rows}


def layer_norm(values):
    mean_val = lax.optimization_barrier(jnp.mean(values, axis=-1, keepdims=True))
    centred = values - mean_val
    variance = lax.optimization_barrier(jnp.mean(centred * centred, axis=-1, keepdims=True))
    return centred * lax.rsqrt(variance + 1e-06)

def head_attention(operands):
    head_queries, head_keys, head_values = operands
    scores = jnp.dot(head_queries, head_keys.T, preferred_element_type=jnp.float32) * (1.0 / math.sqrt(HD))
    scores = scores - lax.optimization_barrier(jnp.max(scores, axis=-1, keepdims=True))
    exponent = jnp.exp(scores)
    weights = (exponent / lax.optimization_barrier(jnp.sum(exponent, axis=-1, keepdims=True))).astype(jnp.bfloat16)
    return jnp.dot(weights, head_values, preferred_element_type=jnp.float32).astype(jnp.bfloat16)

def split_heads(tensor):
    return tensor.reshape(FRAMES, FTOK, H, HD).transpose(0, 2, 1, 3).reshape(FRAMES * H, FTOK, HD)

def reference(stream, queries, key_vectors, value_vectors, modulation, output_weight, output_bias, router_weight, expand_weight, expand_bias, reduce_weight, reduce_bias, counts, picked_rows):
    attended = lax.map(head_attention, (split_heads(queries), split_heads(key_vectors), split_heads(value_vectors)))
    attended = attended.reshape(FRAMES, H, FTOK, HD).transpose(0, 2, 1, 3).reshape(FRAMES * FTOK, D)
    projected = jnp.dot(attended, output_weight, preferred_element_type=jnp.float32) + output_bias
    projected = projected.reshape(FRAMES, FTOK, D)
    residual = (stream.astype(jnp.float32) + modulation[:, 0:1, :] * projected).astype(jnp.bfloat16)
    normed = layer_norm(residual.astype(jnp.float32)) * (1.0 + modulation[:, 2:3, :]) + modulation[:, 1:2, :]
    normed = normed.astype(jnp.bfloat16)
    gate_values = jax.nn.sigmoid(jnp.dot(normed.reshape(FRAMES * FTOK, D), router_weight, preferred_element_type=jnp.float32)).reshape(FRAMES, FTOK, EXPERTS)
    slot_ids = jnp.arange(BLK, dtype=jnp.int32)
    in_use_all = slot_ids[None, None, :] < counts[:, :, None]
    frame_ids = jnp.arange(FRAMES, dtype=jnp.int32)[:, None]

    def one_expert(total, operands):
        expert_id, row_index, in_use, expand_one, expand_bias_one, reduce_one, reduce_bias_one = operands
        chosen = normed[frame_ids, row_index]
        chosen = jnp.where(in_use[:, :, None], chosen, jnp.zeros_like(chosen)).reshape(FRAMES * BLK, D)
        hidden = jax.nn.gelu(jnp.dot(chosen, expand_one, preferred_element_type=jnp.float32) + expand_bias_one, approximate=True).astype(jnp.bfloat16)
        expert_out = (jnp.dot(hidden, reduce_one, preferred_element_type=jnp.float32) + reduce_bias_one).astype(jnp.bfloat16)
        mix_weight = gate_values[frame_ids, row_index, expert_id]
        mix_weight = jnp.where(in_use, mix_weight, jnp.zeros_like(mix_weight)).astype(jnp.bfloat16)
        term = mix_weight.astype(jnp.float32)[:, :, None] * expert_out.reshape(FRAMES, BLK, D).astype(jnp.float32)
        total = total.at[frame_ids, row_index].add(term)
        return (total, None)
    expert_ids = jnp.arange(EXPERTS, dtype=jnp.int32)
    expert_mix, unused = lax.scan(one_expert, jnp.zeros((FRAMES, FTOK, D), jnp.float32), (expert_ids, picked_rows, in_use_all, expand_weight, expand_bias, reduce_weight, reduce_bias))
    return (residual.astype(jnp.float32) + modulation[:, 3:4, :] * expert_mix).astype(jnp.bfloat16)
```

```python
import math

import jax
import jax.numpy as jnp
from jax import lax
from jax.experimental import pallas as pl
from jax.experimental.pallas import tpu as pltpu
from jax.sharding import PartitionSpec as P

H = 16
HD = 72
CAP = 256
BF = jnp.bfloat16
F32 = jnp.float32


def dot(a, b, ca, cb):
    return lax.dot_general(a, b, (((ca,), (cb,)), ((), ())), preferred_element_type=F32)


MESH = pl.DeviceIdType.MESH


def gelu(x):
    return 0.5 * x * (1.0 + jnp.tanh(math.sqrt(2.0 / math.pi) * (x + 0.044715 * (x * x * x))))


LANES = 128


def packed_shape(slots, rest):
    if LANES % rest == 0 and slots % (LANES // rest) == 0 and slots * rest // LANES % 8 == 0:
        return (slots * rest // LANES, LANES)
    return (slots, rest)


def put_block(ref, at, x, slots):
    rest = x.shape[1]
    if ref.shape[1:] == (slots, rest):
        ref[at] = x.astype(BF)
        return
    high = slots * rest // LANES
    parts = [x[i * high : (i + 1) * high] for i in range(LANES // rest)]
    ref[at] = jnp.concatenate(parts, axis=1).astype(BF)


def get_block(ref, at, slots, rest):
    if ref.shape[1:] == (slots, rest):
        return ref[at].astype(F32)
    packed = ref[at].astype(F32)
    parts = [packed[:, i * rest : (i + 1) * rest] for i in range(LANES // rest)]
    return jnp.concatenate(parts, axis=0)


def partners(me, size):
    bits = size.bit_length() - 1
    if 1 << bits != size:
        return [lax.rem(me + d, size) for d in range(1, size)], [
            lax.rem(me + size - d, size) for d in range(1, size)
        ]
    digit = [lax.rem(lax.div(me, 1 << b), 2) for b in range(bits)]
    flipped = [
        sum((1 - digit[b] if d >> b & 1 else digit[b]) * (1 << b) for b in range(bits))
        for d in range(size - 1, 0, -1)
    ]
    return flipped, flipped


def layer_kernel(
    q_ref,
    k_ref,
    v_ref,
    stream_ref,
    mod_ref,
    out_bias_ref,
    router_ref,
    expand_bias_ref,
    reduce_bias_row,
    own_counts_ref,
    picked_ref,
    wo_hbm,
    we_hbm,
    wr_hbm,
    o_ref,
    wo,
    we,
    wr,
    qkv_out,
    qkv_in,
    att_out,
    att_in,
    picks,
    mixers,
    packs,
    packs_turned,
    gate_out,
    gate_in,
    bias_tiles,
    bias_columns,
    counts_ref,
    count_in,
    wide_bufs,
    rest_bufs,
    local_sem,
    head_send,
    head_recv,
    tok_send,
    tok_recv,
    frame_send,
    frame_recv,
):
    shards, heads, _, tokens = att_in.shape
    cols = heads * HD
    full, rest = cols // LANES, cols % LANES
    frames = count_in.shape[0]
    experts = gate_in.shape[1]
    slots = picks.shape[0] // experts
    frame_tokens = shards * tokens
    size = {"tok": shards, "frame": frames}
    me = {"tok": lax.axis_index("tok"), "frame": lax.axis_index("frame")}
    sems = {
        "tok": (tok_send, tok_recv),
        "frame": (frame_send, frame_recv),
        "head": (head_send, head_recv),
    }
    size["head"], me["head"] = size["tok"], me["tok"]
    real = {"tok": "tok", "frame": "frame", "head": "tok"}
    to = {axis: partners(me[axis], size[axis]) for axis in ("tok", "frame")}
    to["head"] = to["tok"]
    tok, frame = me["tok"], me["frame"]

    barrier = pltpu.get_barrier_semaphore()
    for axis in ("frame", "tok"):
        for p in to[axis][0]:
            pl.semaphore_signal(barrier, inc=1, device_id={axis: p}, device_id_type=MESH)

    loads = [
        pltpu.make_async_copy(src, dst, local_sem.at[i])
        for i, (src, dst) in enumerate(((wo_hbm, wo), (we_hbm, we), (wr_hbm, wr)))
    ]
    for load in loads:
        load.start()

    def copy(axis, phase, src, dst, to, slot):
        send, recv = sems[axis]
        return pltpu.make_async_remote_copy(
            src_ref=src,
            dst_ref=dst.at[slot],
            send_sem=send.at[phase, to],
            recv_sem=recv.at[phase, slot],
            device_id={real[axis]: to},
            device_id_type=MESH,
        )

    sent = []

    def send_to(axis, phase, source, dst, p):
        made = copy(axis, phase, source(p), dst, p, me[axis])
        made.start()
        sent.append(made)

    def send_all(axis, phase, source, dst):
        for p in to[axis][0]:
            send_to(axis, phase, source, dst, p)

    def take(axis, phase, source, dst, q):
        copy(axis, phase, source(q), dst, q, q).wait_recv()

    def take_all(axis, phase, source, dst):
        for q in to[axis][1]:
            take(axis, phase, source, dst, q)

    for e in range(experts):
        counts_ref[e] = jnp.broadcast_to(own_counts_ref[:, e : e + 1], (8, 128))
    count_in[frame] = counts_ref[frame]

    def part(t, h):
        return (t * heads + h, lambda p: qkv_out.at[t, p, h], qkv_in.at[t, :, h])

    for t, ref in enumerate((k_ref, v_ref, q_ref)):
        turned = ref[...].astype(F32).T
        for h in range(heads):
            for s in range(shards):
                base = s * cols + h * HD
                qkv_out[t, s, h] = turned[base : base + HD].astype(BF)
    pl.semaphore_wait(barrier, shards + frames - 2)
    for h in range(heads):
        for t in range(3):
            send_all("head", *part(t, h))
    send_all("frame", 0, lambda p: counts_ref.at[p], count_in)
    for t in range(3):
        qkv_in[t, tok] = qkv_out[t, tok]

    token = lax.broadcasted_iota(jnp.int32, (slots, frame_tokens), 1)
    spots = []
    for e in range(experts):
        used = lax.broadcasted_iota(jnp.int32, (1, slots), 1) < counts_ref[e][0:1, 0:slots]
        spot = jnp.where(used, picked_ref[e], -1)
        column = jnp.broadcast_to(spot.astype(F32), (128, slots)).T[:, 0:1].astype(jnp.int32)
        picks[e * slots : (e + 1) * slots] = jnp.where(column == token, 1.0, 0.0).astype(BF)
        spots.append(spot)
    spots = jnp.concatenate(spots, axis=1)
    for s in range(shards):
        token = lax.broadcasted_iota(jnp.int32, (tokens, experts * slots), 0) + s * tokens
        mixers[s] = jnp.where(spots == token, 1.0, 0.0).astype(BF)
    for i in range(full):
        for s in range(shards):
            base = (i * shards + s) * LANES
            bias_tiles[i, s] = jnp.broadcast_to(reduce_bias_row[:, base : base + LANES], (8, LANES))
    wide = full * shards * LANES
    if rest:
        turned = jnp.broadcast_to(reduce_bias_row[:, wide:], (8, shards * rest)).T
        for s in range(shards):
            bias_columns[s] = turned[s * rest : (s + 1) * rest, 0:1]

    scale = math.log2(math.e) / math.sqrt(HD)
    for h in range(heads):
        for t in range(2):
            take_all("head", *part(t, h))
        keys = jnp.concatenate([qkv_in[0, s, h] for s in range(shards)], axis=1).T
        values = jnp.concatenate([qkv_in[1, s, h] for s in range(shards)], axis=1)

        def block(i, carry):
            j = lax.rem(tok + i, shards)

            @pl.when(i > 0)
            def _():
                take("head", *part(2, h), j)

            scores = dot(keys, qkv_in[2, j, h], 1, 0)
            top = jnp.max(scores, axis=0, keepdims=True)
            powers = jnp.exp2((scores - top) * scale)
            denominator = jnp.sum(powers, axis=0, keepdims=True)
            out = dot(values, powers.astype(BF), 1, 0)
            att_out[j, h] = (out / denominator).astype(BF)

            @pl.when(i > 0)
            def _():
                copy("head", 3 * heads + h, att_out.at[j, h], att_in.at[:, h], j, tok).start()

            return carry

        lax.fori_loop(0, shards, block, 0)
        att_in[tok, h] = att_out[tok, h]
        sent.extend(
            copy("head", 3 * heads + h, att_out.at[p, h], att_in.at[:, h], p, tok)
            for p in to["head"][0]
        )

    take_all("frame", 0, lambda p: counts_ref.at[p], count_in)
    slot = lax.broadcasted_iota(jnp.int32, (1, slots), 1)
    turned_row = lax.broadcasted_iota(jnp.int32, (slots, CAP), 1)
    turned_slot = lax.broadcasted_iota(jnp.int32, (slots, CAP), 0)
    first = jnp.zeros((1, LANES), jnp.int32)
    targets = []
    for g in range(frames):
        number = count_in[g][0:1]
        targets.append(jnp.where(slot < number[:, 0:slots], first[:, 0:slots] + slot, -1))
        high = jnp.concatenate([number] * (CAP // LANES), axis=1)
        low = jnp.concatenate([first] * (CAP // LANES), axis=1)
        chosen = (turned_row == low + turned_slot) & (turned_slot < high)
        packs_turned[g * slots : (g + 1) * slots] = jnp.where(chosen, 1.0, 0.0).astype(BF)
        first = first + number
    row = lax.broadcasted_iota(jnp.int32, (CAP, frames * slots), 0)
    packs[...] = jnp.where(row == jnp.concatenate(targets, axis=1), 1.0, 0.0).astype(BF)
    loads[0].wait()

    def project(q):
        block = jnp.concatenate([att_in[q, h].astype(F32) for h in range(heads)], axis=0)
        return dot(block.T.astype(BF), wo[q], 1, 0)

    projected = project(tok)
    for q in to["head"][1]:
        for h in range(heads):
            take("head", 3 * heads + h, lambda p: att_out.at[p, h], att_in.at[:, h], q)
        projected += project(q)
    projected += out_bias_ref[...].reshape(1, shards * cols)
    residual = (stream_ref[...].astype(F32) + mod_ref[0:1] * projected).astype(BF)
    o_ref[...] = residual
    residual = residual.astype(F32)
    centred = residual - jnp.mean(residual, axis=1, keepdims=True)
    variance = jnp.mean(centred * centred, axis=1, keepdims=True)
    normed = (
        centred * lax.rsqrt(variance + 1e-06) * (1.0 + mod_ref[2:3]) + mod_ref[1:2]
    ).astype(BF)

    normed_out, normed_in, chosen_out, chosen_in, rows_all, part_out, part_in = wide_bufs[:7]
    ret_out, ret_in, mix_out, mix_in = wide_bufs[7:]
    slim_normed_out, slim_normed_in, slim_chosen_out, slim_chosen_in = rest_bufs[:4]
    slim_rows, slim_part_out, slim_part_in, slim_ret_out, slim_ret_in = rest_bufs[4:9]
    slim_mix_out, slim_mix_in = rest_bufs[9:]
    chunks = list(range(full)) + [full] * (rest > 0)
    steps = full + 1

    def chunk(axis, stage, i, wide_from, wide_to, slim_from, slim_to):
        phase = 1 + stage * steps + i
        if i < full:
            return (axis, phase, lambda p: wide_from.at[i, p], wide_to.at[i])
        return (axis, phase, lambda p: slim_from.at[p], slim_to)

    def normed_of(i):
        return chunk("tok", 0, i, normed_out, normed_in, slim_normed_out, slim_normed_in)

    def chosen_of(i):
        return chunk("frame", 0, i, chosen_out, chosen_in, slim_chosen_out, slim_chosen_in)

    def rows_of(i):
        if i < full:
            return ("tok", 1 + steps + i, lambda p: rows_all.at[i, tok], rows_all.at[i])
        return ("tok", 1 + steps + i, lambda p: slim_rows.at[tok], slim_rows)

    def part_of(i):
        return chunk("tok", 2, i, part_out, part_in, slim_part_out, slim_part_in)

    def ret_of(i):
        return chunk("frame", 1, i, ret_out, ret_in, slim_ret_out, slim_ret_in)

    def mix_of(i):
        return chunk("tok", 3, i, mix_out, mix_in, slim_mix_out, slim_mix_in)

    def stacked(ref):
        n, high = ref.shape[0], ref.shape[1]
        if high % 16 == 0:
            return jnp.concatenate([ref[s] for s in range(n)], axis=0)
        return jnp.concatenate([ref[s].astype(F32) for s in range(n)], axis=0).astype(BF)

    def unpacked(ref):
        blocks = [get_block(ref, g, slots, rest) for g in range(ref.shape[0])]
        return jnp.concatenate(blocks, axis=0).astype(BF)

    for i in chunks:
        if i < full:
            for s in range(shards):
                base = (i * shards + s) * LANES
                normed_out[i, s] = normed[:, base : base + LANES]
        else:
            turned = normed[:, wide:].T
            for s in range(shards):
                slim_normed_out[s] = turned[s * rest : (s + 1) * rest]
        send_all(*normed_of(i))
    gates = dot(router_ref[...], normed, 1, 1)
    gate_out[...] = 1.0 / (1.0 + jnp.exp(-gates))
    send_all("tok", 0, lambda p: gate_out, gate_in)
    gate_in[tok] = gate_out[...]

    for i in chunks:
        if i < full:
            normed_in[i, tok] = normed_out[i, tok]
            take_all(*normed_of(i))
            held = normed_in[i].reshape(frame_tokens, LANES)
            chosen = dot(picks[...], held, 1, 0)
            for e in range(experts):
                chosen_out[i, e] = chosen[e * slots : (e + 1) * slots].astype(BF)
            send_all(*chosen_of(i))
            chosen_in[i, frame] = chosen_out[i, frame]
        else:
            slim_normed_in[tok] = slim_normed_out[tok]
            take_all(*normed_of(i))
            held = jnp.concatenate([slim_normed_in[s] for s in range(shards)], axis=1)
            chosen = dot(picks[...], held, 1, 1)
            for e in range(experts):
                put_block(slim_chosen_out, e, chosen[e * slots : (e + 1) * slots], slots)
            send_all(*chosen_of(i))
            slim_chosen_in[frame] = slim_chosen_out[frame]

    take_all("tok", 0, lambda p: gate_out, gate_in)
    owner = lax.broadcasted_iota(jnp.int32, (experts, experts * slots), 1)
    expert = lax.broadcasted_iota(jnp.int32, (experts, experts * slots), 0) * slots
    spread = jnp.where((owner >= expert) & (owner < expert + slots), 1.0, 0.0).astype(BF)
    for s in range(shards):
        mixers[s] = mixers[s] * dot(gate_in[s].astype(BF), spread, 0, 0).astype(BF)

    loads[1].wait()
    hidden = None

    def expand(i, hidden):
        take_all(*rows_of(i))
        if i < full:
            base = i * shards * LANES
            rows = jnp.concatenate([rows_all[i, s] for s in range(shards)], axis=1)
            more = dot(rows, we[base : base + shards * LANES], 1, 0)
        else:
            more = dot(stacked(slim_rows), we[wide:], 0, 0)
        return more if hidden is None else hidden + more

    for at, i in enumerate(chunks):
        take_all(*chosen_of(i))
        if i < full:
            rows = dot(packs[...], chosen_in[i].reshape(frames * slots, LANES), 1, 0)
            rows_all[i, tok] = rows.astype(BF)
        else:
            slim_rows[tok] = dot(packs[...], unpacked(slim_chosen_in), 1, 0).T.astype(BF)
        send_all(*rows_of(i))
        if at:
            hidden = expand(chunks[at - 1], hidden)
    hidden = expand(chunks[-1], hidden)
    hidden = gelu(hidden + expand_bias_ref[...]).astype(BF)
    loads[2].wait()

    for i in chunks:
        if i < full:
            base = i * shards * LANES
            out = dot(hidden, wr[:, base : base + shards * LANES], 1, 0)
            for s in range(shards):
                part_out[i, s] = out[:, s * LANES : (s + 1) * LANES].astype(BF)
        else:
            out = dot(hidden, wr[:, wide:], 1, 0).T
            for s in range(shards):
                slim_part_out[s] = out[s * rest : (s + 1) * rest].astype(BF)
        send_all(*part_of(i))
    for i in chunks:
        if i < full:
            part_in[i, tok] = part_out[i, tok]
            take_all(*part_of(i))
            total = part_in[i, 0].astype(F32)
            for s in range(1, shards):
                total += part_in[i, s].astype(F32)
            out = (total + bias_tiles[i, tok][0:1]).astype(BF)
            back = dot(packs_turned[...], out, 1, 0)
            for g in range(frames):
                ret_out[i, g] = back[g * slots : (g + 1) * slots].astype(BF)
            send_all(*ret_of(i))
            ret_in[i, frame] = ret_out[i, frame]
        else:
            slim_part_in[tok] = slim_part_out[tok]
            take_all(*part_of(i))
            total = slim_part_in[0].astype(F32)
            for s in range(1, shards):
                total += slim_part_in[s].astype(F32)
            out = (total + bias_columns[tok]).astype(BF)
            back = dot(packs_turned[...], out, 1, 1)
            for g in range(frames):
                put_block(slim_ret_out, g, back[g * slots : (g + 1) * slots], slots)
            send_all(*ret_of(i))
            slim_ret_in[frame] = slim_ret_out[frame]

    for i in chunks:
        take_all(*ret_of(i))
        if i < full:
            back = ret_in[i].reshape(experts * slots, LANES)
            for p in to["tok"][0]:
                mix_out[i, p] = dot(mixers[p], back, 1, 0).astype(BF)
                send_to(*mix_of(i), p)
            mix_in[i, tok] = dot(mixers[tok], back, 1, 0).astype(BF)
        else:
            back = unpacked(slim_ret_in)
            for p in to["tok"][0]:
                slim_mix_out[p] = dot(mixers[p], back, 1, 0).T.astype(BF)
                send_to(*mix_of(i), p)
            slim_mix_in[tok] = dot(mixers[tok], back, 1, 0).T.astype(BF)
    for i in chunks:
        take_all(*mix_of(i))
        if i < full:
            for s in range(shards):
                base = (i * shards + s) * LANES
                at = slice(base, base + LANES)
                mix = mix_in[i, s].astype(F32)
                o_ref[:, at] = (o_ref[:, at].astype(F32) + mod_ref[3:4, at] * mix).astype(BF)
        else:
            mix = stacked(slim_mix_in).astype(F32).T
            at = slice(wide, wide + shards * rest)
            o_ref[:, at] = (o_ref[:, at].astype(F32) + mod_ref[3:4, at] * mix).astype(BF)
    for made in sent:
        made.wait_send()


def per_device(
    stream,
    queries,
    key_vectors,
    value_vectors,
    modulation,
    output_weight,
    output_bias,
    router_weight,
    expand_weight,
    expand_bias,
    reduce_weight,
    reduce_bias,
    counts,
    picked_rows,
):
    shards = lax.axis_size("tok")
    frames = lax.axis_size("frame")
    tokens = stream.shape[1]
    width = stream.shape[2]
    hidden = expand_weight.shape[2]
    cols = width // shards
    heads = H // shards
    experts, _, slots = picked_rows.shape
    full, rest = cols // LANES, cols % LANES
    wide, slim = max(full, 1), max(rest, 8)
    steps = full + 1

    vmem = pl.BlockSpec(memory_space=pltpu.VMEM)
    hbm = pl.BlockSpec(memory_space=pl.ANY)
    by_token = pltpu.VMEM((wide, shards, tokens, LANES), BF)
    by_frame = pltpu.VMEM((wide, frames, slots, LANES), BF)
    by_row = pltpu.VMEM((wide, shards, CAP, LANES), BF)
    slim_token = pltpu.VMEM((shards, slim, tokens), BF)
    slim_frame = pltpu.VMEM((frames, *packed_shape(slots, slim)), BF)
    slim_row = pltpu.VMEM((shards, slim, CAP), BF)
    layer_out = pl.pallas_call(
        layer_kernel,
        out_shape=jax.ShapeDtypeStruct((tokens, width), BF),
        in_specs=[vmem] * 11 + [hbm] * 3,
        out_specs=vmem,
        scratch_shapes=[
            pltpu.VMEM((shards, cols, width), BF),
            pltpu.VMEM((width, hidden), BF),
            pltpu.VMEM((hidden, width), BF),
            pltpu.VMEM((3, shards, heads, HD, tokens), BF),
            pltpu.VMEM((3, shards, heads, HD, tokens), BF),
            pltpu.VMEM((shards, heads, HD, tokens), BF),
            pltpu.VMEM((shards, heads, HD, tokens), BF),
            pltpu.VMEM((experts * slots, shards * tokens), BF),
            pltpu.VMEM((shards, tokens, experts * slots), BF),
            pltpu.VMEM((CAP, frames * slots), BF),
            pltpu.VMEM((frames * slots, CAP), BF),
            pltpu.VMEM((experts, tokens), F32),
            pltpu.VMEM((shards, experts, tokens), F32),
            pltpu.VMEM((wide, shards, 8, LANES), F32),
            pltpu.VMEM((shards, slim, 1), F32),
            pltpu.VMEM((frames, 8, 128), jnp.int32),
            pltpu.VMEM((frames, 8, 128), jnp.int32),
            [by_token] * 2 + [by_frame] * 2 + [by_row] * 3 + [by_frame] * 2 + [by_token] * 2,
            [slim_token] * 2 + [slim_frame] * 2 + [slim_row] * 3 + [slim_frame] * 2 + [slim_token] * 2,
            pltpu.SemaphoreType.DMA((3,)),
            pltpu.SemaphoreType.DMA((4 * heads, shards)),
            pltpu.SemaphoreType.DMA((4 * heads, shards)),
            pltpu.SemaphoreType.DMA((1 + 4 * steps, shards)),
            pltpu.SemaphoreType.DMA((1 + 4 * steps, shards)),
            pltpu.SemaphoreType.DMA((1 + 2 * steps, frames)),
            pltpu.SemaphoreType.DMA((1 + 2 * steps, frames)),
        ],
        compiler_params=pltpu.CompilerParams(
            collective_id=1, has_side_effects=True, vmem_limit_bytes=60 << 20
        ),
    )(
        queries[0],
        key_vectors[0],
        value_vectors[0],
        stream[0],
        modulation[0],
        output_bias,
        router_weight.T,
        expand_bias,
        reduce_bias,
        counts.T,
        picked_rows,
        output_weight.reshape(shards, cols, width),
        expand_weight[0],
        reduce_weight[0],
    )
    return layer_out[None]


def solution(mesh):
    return jax.shard_map(
        per_device,
        mesh=mesh,
        in_specs=(
            P("frame", "tok", None),
            P("frame", "tok", None),
            P("frame", "tok", None),
            P("frame", "tok", None),
            P("frame", None, None),
            P(),
            P(),
            P(),
            P("frame", None, "tok"),
            P("frame", "tok"),
            P("frame", "tok", None),
            P("frame", None),
            P(None, "frame"),
            P(None, "frame", None),
        ),
        out_specs=P("frame", "tok", None),
        check_vma=False,
    )
```

```python
import math

import jax
import jax.numpy as jnp
from jax import lax
from jax.experimental import pallas as pl
from jax.experimental.pallas import tpu as pltpu
from jax.sharding import PartitionSpec as P

H = 16
HD = 72
CAP = 256
BF = jnp.bfloat16
F32 = jnp.float32


def dot(a, b, ca, cb):
    return lax.dot_general(a, b, (((ca,), (cb,)), ((), ())), preferred_element_type=F32)


MESH = pl.DeviceIdType.MESH


def gelu(x):
    return 0.5 * x * (1.0 + jnp.tanh(math.sqrt(2.0 / math.pi) * (x + 0.044715 * (x * x * x))))


LANES = 128


def packed_shape(slots, rest):
    if LANES % rest == 0 and slots % (LANES // rest) == 0 and slots * rest // LANES % 8 == 0:
        return (slots * rest // LANES, LANES)
    return (slots, rest)


def put_block(ref, at, x, slots):
    rest = x.shape[1]
    if ref.shape[1:] == (slots, rest):
        ref[at] = x.astype(BF)
        return
    high = slots * rest // LANES
    parts = [x[i * high : (i + 1) * high] for i in range(LANES // rest)]
    ref[at] = jnp.concatenate(parts, axis=1).astype(BF)


def get_block(ref, at, slots, rest):
    if ref.shape[1:] == (slots, rest):
        return ref[at].astype(F32)
    packed = ref[at].astype(F32)
    parts = [packed[:, i * rest : (i + 1) * rest] for i in range(LANES // rest)]
    return jnp.concatenate(parts, axis=0)


def partners(me, size):
    bits = size.bit_length() - 1
    if 1 << bits != size:
        return [lax.rem(me + d, size) for d in range(1, size)], [
            lax.rem(me + size - d, size) for d in range(1, size)
        ]
    digit = [lax.rem(lax.div(me, 1 << b), 2) for b in range(bits)]
    flipped = [
        sum((1 - digit[b] if d >> b & 1 else digit[b]) * (1 << b) for b in range(bits))
        for d in range(size - 1, 0, -1)
    ]
    return flipped, flipped


def layer_kernel(
    *refs,
):
    sources, o_ref, held_inputs = refs[:14], refs[14], refs[15:29]
    (
        q_ref,
        k_ref,
        v_ref,
        stream_ref,
        mod_ref,
        out_bias_ref,
        router_ref,
        expand_bias_ref,
        reduce_bias_row,
        own_counts_ref,
        picked_ref,
        wo,
        we,
        wr,
    ) = held_inputs
    (
        qkv_out,
        qkv_in,
        att_out,
        att_in,
        picks,
        mixers,
        packs,
        packs_turned,
        gate_out,
        gate_in,
        bias_tiles,
        bias_columns,
        counts_ref,
        count_in,
        wide_bufs,
        rest_bufs,
        local_sem,
        qkv_send,
        kv_recv,
        q_recv,
        att_send,
        att_recv,
        tok_send,
        tok_recv,
        frame_send,
        frame_recv,
    ) = refs[29:]
    shards, heads, _, tokens = att_in.shape
    cols = heads * HD
    full, rest = cols // LANES, cols % LANES
    frames = count_in.shape[0]
    experts = gate_in.shape[1]
    slots = picks.shape[0] // experts
    frame_tokens = shards * tokens
    size = {"tok": shards, "frame": frames}
    me = {"tok": lax.axis_index("tok"), "frame": lax.axis_index("frame")}
    sems = {"tok": (tok_send, tok_recv), "frame": (frame_send, frame_recv)}
    to = {axis: partners(me[axis], size[axis]) for axis in ("tok", "frame")}
    tok, frame = me["tok"], me["frame"]

    barrier = pltpu.get_barrier_semaphore()
    for axis in ("frame", "tok"):
        for p in to[axis][0]:
            pl.semaphore_signal(barrier, inc=1, device_id={axis: p}, device_id_type=MESH)

    loads = [
        pltpu.make_async_copy(src, dst, local_sem.at[i])
        for i, (src, dst) in enumerate(zip(sources, held_inputs))
    ]
    for i in (1, 2, 0, 9, 10, 8, 3, 4, 5, 6, 7, 11, 12, 13):
        loads[i].start()

    def remote(src, dst, send_sem, recv_sem, axis, p):
        return pltpu.make_async_remote_copy(
            src_ref=src,
            dst_ref=dst,
            send_sem=send_sem,
            recv_sem=recv_sem,
            device_id={axis: p},
            device_id_type=MESH,
        )

    unsent = []

    def sends_of(ref, sem, axis):
        unsent.append(remote(ref, ref, sem, sem, axis, me[axis]))

    def send_to(axis, phase, source, dst, p):
        send, recv = sems[axis]
        remote(source(p), dst.at[me[axis]], send.at[phase], recv.at[phase], axis, p).start()

    def send_all(axis, phase, source, dst):
        for p in to[axis][0]:
            send_to(axis, phase, source, dst, p)

    def take_all(axis, phase, source, dst):
        send, recv = sems[axis]
        come = dst.at[0 : size[axis] - 1]
        remote(come, come, send.at[phase], recv.at[phase], axis, me[axis]).wait_recv()
        sends_of(come, send.at[phase], axis)

    loads[9].wait()
    for e in range(experts):
        counts_ref[e] = jnp.broadcast_to(own_counts_ref[:, e : e + 1], (8, 128))
    count_in[frame] = counts_ref[frame]

    for t, ref in enumerate((k_ref, v_ref, q_ref)):
        loads[(1, 2, 0)[t]].wait()
        turned = ref[...].astype(F32).T
        for h in range(heads):
            for s in range(shards):
                base = s * cols + h * HD
                qkv_out[t, s, h] = turned[base : base + HD].astype(BF)
    pl.semaphore_wait(barrier, shards + frames - 2)
    for h in range(heads):
        for t in range(3):
            recv = (q_recv if t == 2 else kv_recv).at[h]
            for p in to["tok"][0]:
                remote(
                    qkv_out.at[t, p, h], qkv_in.at[t, tok, h], qkv_send.at[0], recv, "tok", p
                ).start()
    send_all("frame", 0, lambda p: counts_ref.at[p], count_in)
    for t in range(3):
        qkv_in[t, tok] = qkv_out[t, tok]

    loads[10].wait()
    loads[8].wait()
    token = lax.broadcasted_iota(jnp.int32, (slots, frame_tokens), 1)
    spots = []
    for e in range(experts):
        used = lax.broadcasted_iota(jnp.int32, (1, slots), 1) < counts_ref[e][0:1, 0:slots]
        spot = jnp.where(used, picked_ref[e], -1)
        column = jnp.broadcast_to(spot.astype(F32), (128, slots)).T[:, 0:1].astype(jnp.int32)
        picks[e * slots : (e + 1) * slots] = jnp.where(column == token, 1.0, 0.0).astype(BF)
        spots.append(spot)
    spots = jnp.concatenate(spots, axis=1)
    for s in range(shards):
        token = lax.broadcasted_iota(jnp.int32, (tokens, experts * slots), 0) + s * tokens
        mixers[s] = jnp.where(spots == token, 1.0, 0.0).astype(BF)
    for i in range(full):
        for s in range(shards):
            base = (i * shards + s) * LANES
            bias_tiles[i, s] = jnp.broadcast_to(reduce_bias_row[:, base : base + LANES], (8, LANES))
    wide = full * shards * LANES
    if rest:
        turned = jnp.broadcast_to(reduce_bias_row[:, wide:], (8, shards * rest)).T
        for s in range(shards):
            bias_columns[s] = turned[s * rest : (s + 1) * rest, 0:1]

    scale = math.log2(math.e) / math.sqrt(HD)
    others = shards - 1

    def far(i):
        if 1 << shards.bit_length() - 1 != shards:
            return lax.rem(tok + i, shards)
        flip, p = lax.rem(shards - i, shards), 0
        for b in range(shards.bit_length() - 1):
            mine, turn = (lax.rem(lax.div(x, 1 << b), 2) for x in (tok, flip))
            p += (mine + turn - 2 * mine * turn) * (1 << b)
        return p

    for h in range(heads):
        come = qkv_in.at[0:2, 0:others, h]
        remote(come, come, qkv_send.at[0], kv_recv.at[h], "tok", tok).wait_recv()
        keys = jnp.concatenate([qkv_in[0, s, h] for s in range(shards)], axis=1).T
        values = jnp.concatenate([qkv_in[1, s, h] for s in range(shards)], axis=1)

        def block(i, carry):
            j = far(i)

            @pl.when(i == 1)
            def _():
                come = qkv_in.at[2, 0:others, h]
                remote(come, come, qkv_send.at[0], q_recv.at[h], "tok", tok).wait_recv()

            scores = dot(keys, qkv_in[2, j, h], 1, 0)
            top = jnp.max(scores, axis=0, keepdims=True)
            powers = jnp.exp2((scores - top) * scale)
            denominator = jnp.sum(powers, axis=0, keepdims=True)
            out = dot(values, powers.astype(BF), 1, 0)
            att_out[j, h] = (out / denominator).astype(BF)

            @pl.when(i > 0)
            def _():
                remote(
                    att_out.at[j, h],
                    att_in.at[tok, h],
                    att_send.at[0],
                    att_recv.at[tok],
                    "tok",
                    j,
                ).start()

            return carry

        lax.fori_loop(0, shards, block, 0)
        att_in[tok, h] = att_out[tok, h]
    sends_of(qkv_out.at[:, 0:others], qkv_send.at[0], "tok")
    sends_of(att_out.at[0:others], att_send.at[0], "tok")

    take_all("frame", 0, lambda p: counts_ref.at[p], count_in)
    slot = lax.broadcasted_iota(jnp.int32, (1, slots), 1)
    turned_row = lax.broadcasted_iota(jnp.int32, (slots, CAP), 1)
    turned_slot = lax.broadcasted_iota(jnp.int32, (slots, CAP), 0)
    first = jnp.zeros((1, LANES), jnp.int32)
    targets = []
    for g in range(frames):
        number = count_in[g][0:1]
        targets.append(jnp.where(slot < number[:, 0:slots], first[:, 0:slots] + slot, -1))
        high = jnp.concatenate([number] * (CAP // LANES), axis=1)
        low = jnp.concatenate([first] * (CAP // LANES), axis=1)
        chosen = (turned_row == low + turned_slot) & (turned_slot < high)
        packs_turned[g * slots : (g + 1) * slots] = jnp.where(chosen, 1.0, 0.0).astype(BF)
        first = first + number
    row = lax.broadcasted_iota(jnp.int32, (CAP, frames * slots), 0)
    packs[...] = jnp.where(row == jnp.concatenate(targets, axis=1), 1.0, 0.0).astype(BF)
    loads[11].wait()

    def project(q):
        block = jnp.concatenate([att_in[q, h].astype(F32) for h in range(heads)], axis=0)
        return dot(block.T.astype(BF), wo[q], 1, 0)

    projected = project(tok)
    for q in to["tok"][1][::-1]:
        remote(
            att_in.at[q], att_in.at[q], att_send.at[0], att_recv.at[q], "tok", tok
        ).wait_recv()
        projected += project(q)
    for i in (3, 4, 5, 6):
        loads[i].wait()
    projected += out_bias_ref[...].reshape(1, shards * cols)
    residual = (stream_ref[...].astype(F32) + mod_ref[0:1] * projected).astype(BF)
    o_ref[...] = residual
    residual = residual.astype(F32)
    centred = residual - jnp.mean(residual, axis=1, keepdims=True)
    variance = jnp.mean(centred * centred, axis=1, keepdims=True)
    normed = (
        centred * lax.rsqrt(variance + 1e-06) * (1.0 + mod_ref[2:3]) + mod_ref[1:2]
    ).astype(BF)

    normed_out, normed_in, chosen_out, chosen_in, rows_all, part_out, part_in = wide_bufs[:7]
    ret_out, ret_in, mix_out, mix_in = wide_bufs[7:]
    slim_normed_out, slim_normed_in, slim_chosen_out, slim_chosen_in = rest_bufs[:4]
    slim_rows, slim_part_out, slim_part_in, slim_ret_out, slim_ret_in = rest_bufs[4:9]
    slim_mix_out, slim_mix_in = rest_bufs[9:]
    chunks = list(range(full)) + [full] * (rest > 0)
    steps = full + 1

    def chunk(axis, stage, i, wide_from, wide_to, slim_from, slim_to):
        phase = 1 + stage * steps + i
        if i < full:
            return (axis, phase, lambda p: wide_from.at[i, p], wide_to.at[i])
        return (axis, phase, lambda p: slim_from.at[p], slim_to)

    def normed_of(i):
        return chunk("tok", 0, i, normed_out, normed_in, slim_normed_out, slim_normed_in)

    def chosen_of(i):
        return chunk("frame", 0, i, chosen_out, chosen_in, slim_chosen_out, slim_chosen_in)

    def rows_of(i):
        if i < full:
            return ("tok", 1 + steps + i, lambda p: rows_all.at[i, tok], rows_all.at[i])
        return ("tok", 1 + steps + i, lambda p: slim_rows.at[tok], slim_rows)

    def part_of(i):
        return chunk("tok", 2, i, part_out, part_in, slim_part_out, slim_part_in)

    def ret_of(i):
        return chunk("frame", 1, i, ret_out, ret_in, slim_ret_out, slim_ret_in)

    def mix_of(i):
        return chunk("tok", 3, i, mix_out, mix_in, slim_mix_out, slim_mix_in)

    def stacked(ref):
        n, high = ref.shape[0], ref.shape[1]
        if high % 16 == 0:
            return jnp.concatenate([ref[s] for s in range(n)], axis=0)
        return jnp.concatenate([ref[s].astype(F32) for s in range(n)], axis=0).astype(BF)

    def unpacked(ref):
        blocks = [get_block(ref, g, slots, rest) for g in range(ref.shape[0])]
        return jnp.concatenate(blocks, axis=0).astype(BF)

    for i in chunks:
        if i < full:
            for s in range(shards):
                base = (i * shards + s) * LANES
                normed_out[i, s] = normed[:, base : base + LANES]
        else:
            turned = normed[:, wide:].T
            for s in range(shards):
                slim_normed_out[s] = turned[s * rest : (s + 1) * rest]
        send_all(*normed_of(i))
    gates = dot(router_ref[...], normed, 1, 1)
    gate_out[...] = 1.0 / (1.0 + jnp.exp(-gates))
    send_all("tok", 0, lambda p: gate_out, gate_in)
    gate_in[tok] = gate_out[...]

    for i in chunks:
        if i < full:
            normed_in[i, tok] = normed_out[i, tok]
            take_all(*normed_of(i))
            held = normed_in[i].reshape(frame_tokens, LANES)
            chosen = dot(picks[...], held, 1, 0)
            for e in range(experts):
                chosen_out[i, e] = chosen[e * slots : (e + 1) * slots].astype(BF)
            send_all(*chosen_of(i))
            chosen_in[i, frame] = chosen_out[i, frame]
        else:
            slim_normed_in[tok] = slim_normed_out[tok]
            take_all(*normed_of(i))
            held = jnp.concatenate([slim_normed_in[s] for s in range(shards)], axis=1)
            chosen = dot(picks[...], held, 1, 1)
            for e in range(experts):
                put_block(slim_chosen_out, e, chosen[e * slots : (e + 1) * slots], slots)
            send_all(*chosen_of(i))
            slim_chosen_in[frame] = slim_chosen_out[frame]

    take_all("tok", 0, lambda p: gate_out, gate_in)
    owner = lax.broadcasted_iota(jnp.int32, (experts, experts * slots), 1)
    expert = lax.broadcasted_iota(jnp.int32, (experts, experts * slots), 0) * slots
    spread = jnp.where((owner >= expert) & (owner < expert + slots), 1.0, 0.0).astype(BF)
    for s in range(shards):
        mixers[s] = mixers[s] * dot(gate_in[s].astype(BF), spread, 0, 0).astype(BF)

    loads[12].wait()
    loads[7].wait()
    hidden = None

    def expand(i, hidden):
        take_all(*rows_of(i))
        if i < full:
            base = i * shards * LANES
            rows = jnp.concatenate([rows_all[i, s] for s in range(shards)], axis=1)
            more = dot(rows, we[base : base + shards * LANES], 1, 0)
        else:
            more = dot(stacked(slim_rows), we[wide:], 0, 0)
        return more if hidden is None else hidden + more

    for i in chunks:
        take_all(*chosen_of(i))
        if i < full:
            rows = dot(packs[...], chosen_in[i].reshape(frames * slots, LANES), 1, 0)
            rows_all[i, tok] = rows.astype(BF)
        else:
            slim_rows[tok] = dot(packs[...], unpacked(slim_chosen_in), 1, 0).T.astype(BF)
        send_all(*rows_of(i))
    for i in chunks:
        hidden = expand(i, hidden)
    hidden = gelu(hidden + expand_bias_ref[...]).astype(BF)
    loads[13].wait()

    for i in chunks:
        if i < full:
            base = i * shards * LANES
            out = dot(hidden, wr[:, base : base + shards * LANES], 1, 0)
            for s in range(shards):
                part_out[i, s] = out[:, s * LANES : (s + 1) * LANES].astype(BF)
        else:
            out = dot(hidden, wr[:, wide:], 1, 0).T
            for s in range(shards):
                slim_part_out[s] = out[s * rest : (s + 1) * rest].astype(BF)
        send_all(*part_of(i))
    for i in chunks:
        if i < full:
            part_in[i, tok] = part_out[i, tok]
            take_all(*part_of(i))
            total = part_in[i, 0].astype(F32)
            for s in range(1, shards):
                total += part_in[i, s].astype(F32)
            out = (total + bias_tiles[i, tok][0:1]).astype(BF)
            back = dot(packs_turned[...], out, 1, 0)
            for g in range(frames):
                ret_out[i, g] = back[g * slots : (g + 1) * slots].astype(BF)
            send_all(*ret_of(i))
            ret_in[i, frame] = ret_out[i, frame]
        else:
            slim_part_in[tok] = slim_part_out[tok]
            take_all(*part_of(i))
            total = slim_part_in[0].astype(F32)
            for s in range(1, shards):
                total += slim_part_in[s].astype(F32)
            out = (total + bias_columns[tok]).astype(BF)
            back = dot(packs_turned[...], out, 1, 1)
            for g in range(frames):
                put_block(slim_ret_out, g, back[g * slots : (g + 1) * slots], slots)
            send_all(*ret_of(i))
            slim_ret_in[frame] = slim_ret_out[frame]

    for i in chunks:
        take_all(*ret_of(i))
        if i < full:
            back = ret_in[i].reshape(experts * slots, LANES)
            for p in to["tok"][0]:
                mix_out[i, p] = dot(mixers[p], back, 1, 0).astype(BF)
                send_to(*mix_of(i), p)
            mix_in[i, tok] = dot(mixers[tok], back, 1, 0).astype(BF)
        else:
            back = unpacked(slim_ret_in)
            for p in to["tok"][0]:
                slim_mix_out[p] = dot(mixers[p], back, 1, 0).T.astype(BF)
                send_to(*mix_of(i), p)
            slim_mix_in[tok] = dot(mixers[tok], back, 1, 0).T.astype(BF)
    for i in chunks:
        take_all(*mix_of(i))
        if i < full:
            for s in range(shards):
                base = (i * shards + s) * LANES
                at = slice(base, base + LANES)
                mix = mix_in[i, s].astype(F32)
                o_ref[:, at] = (o_ref[:, at].astype(F32) + mod_ref[3:4, at] * mix).astype(BF)
        else:
            mix = stacked(slim_mix_in).astype(F32).T
            at = slice(wide, wide + shards * rest)
            o_ref[:, at] = (o_ref[:, at].astype(F32) + mod_ref[3:4, at] * mix).astype(BF)
    for made in unsent:
        made.wait_send()


def per_device(
    stream,
    queries,
    key_vectors,
    value_vectors,
    modulation,
    output_weight,
    output_bias,
    router_weight,
    expand_weight,
    expand_bias,
    reduce_weight,
    reduce_bias,
    counts,
    picked_rows,
):
    shards = lax.axis_size("tok")
    frames = lax.axis_size("frame")
    tokens = stream.shape[1]
    width = stream.shape[2]
    hidden = expand_weight.shape[2]
    cols = width // shards
    heads = H // shards
    experts, _, slots = picked_rows.shape
    full, rest = cols // LANES, cols % LANES
    wide, slim = max(full, 1), max(rest, 8)
    steps = full + 1

    vmem = pl.BlockSpec(memory_space=pltpu.VMEM)
    hbm = pl.BlockSpec(memory_space=pl.ANY)
    by_token = pltpu.VMEM((wide, shards, tokens, LANES), BF)
    by_frame = pltpu.VMEM((wide, frames, slots, LANES), BF)
    by_row = pltpu.VMEM((wide, shards, CAP, LANES), BF)
    slim_token = pltpu.VMEM((shards, slim, tokens), BF)
    slim_frame = pltpu.VMEM((frames, *packed_shape(slots, slim)), BF)
    slim_row = pltpu.VMEM((shards, slim, CAP), BF)
    operands = (
        queries[0],
        key_vectors[0],
        value_vectors[0],
        stream[0],
        modulation[0],
        output_bias,
        router_weight.T,
        expand_bias,
        reduce_bias,
        counts.T,
        picked_rows,
        output_weight.reshape(shards, cols, width),
        expand_weight[0],
        reduce_weight[0],
    )
    layer_out = pl.pallas_call(
        layer_kernel,
        out_shape=jax.ShapeDtypeStruct((tokens, width), BF),
        in_specs=[hbm] * 14,
        out_specs=vmem,
        scratch_shapes=[
            *[pltpu.VMEM(x.shape, x.dtype) for x in operands],
            pltpu.VMEM((3, shards, heads, HD, tokens), BF),
            pltpu.VMEM((3, shards, heads, HD, tokens), BF),
            pltpu.VMEM((shards, heads, HD, tokens), BF),
            pltpu.VMEM((shards, heads, HD, tokens), BF),
            pltpu.VMEM((experts * slots, shards * tokens), BF),
            pltpu.VMEM((shards, tokens, experts * slots), BF),
            pltpu.VMEM((CAP, frames * slots), BF),
            pltpu.VMEM((frames * slots, CAP), BF),
            pltpu.VMEM((experts, tokens), F32),
            pltpu.VMEM((shards, experts, tokens), F32),
            pltpu.VMEM((wide, shards, 8, LANES), F32),
            pltpu.VMEM((shards, slim, 1), F32),
            pltpu.VMEM((frames, 8, 128), jnp.int32),
            pltpu.VMEM((frames, 8, 128), jnp.int32),
            [by_token] * 2 + [by_frame] * 2 + [by_row] * 3 + [by_frame] * 2 + [by_token] * 2,
            [slim_token] * 2 + [slim_frame] * 2 + [slim_row] * 3 + [slim_frame] * 2 + [slim_token] * 2,
            pltpu.SemaphoreType.DMA((len(operands),)),
            pltpu.SemaphoreType.DMA((1,)),
            pltpu.SemaphoreType.DMA((heads,)),
            pltpu.SemaphoreType.DMA((heads,)),
            pltpu.SemaphoreType.DMA((1,)),
            pltpu.SemaphoreType.DMA((shards,)),
            pltpu.SemaphoreType.DMA((1 + 4 * steps,)),
            pltpu.SemaphoreType.DMA((1 + 4 * steps,)),
            pltpu.SemaphoreType.DMA((1 + 2 * steps,)),
            pltpu.SemaphoreType.DMA((1 + 2 * steps,)),
        ],
        compiler_params=pltpu.CompilerParams(
            collective_id=1, has_side_effects=True, vmem_limit_bytes=60 << 20
        ),
    )(*operands)
    return layer_out[None]


def solution(mesh):
    return jax.shard_map(
        per_device,
        mesh=mesh,
        in_specs=(
            P("frame", "tok", None),
            P("frame", "tok", None),
            P("frame", "tok", None),
            P("frame", "tok", None),
            P("frame", None, None),
            P(),
            P(),
            P(),
            P("frame", None, "tok"),
            P("frame", "tok"),
            P("frame", "tok", None),
            P("frame", None),
            P(None, "frame"),
            P(None, "frame", None),
        ),
        out_specs=P("frame", "tok", None),
        check_vma=False,
    )
```
